256 devices in a mesh: front: 4 (over y), pivot: 8 (over x, core), rows: 8 (over z).
Axes of the slice: x: 4, y: 4, z: 8, core: 2. Of those that a mesh axis runs over, the one named last changes fastest.
Arguments:
- factor: float32 [4, 8, 1024, 8192], P('front', 'pivot', 'rows'), may hold values from -0.0625 to 0.0625
- inv_diag: float32 [4, 8, 1024, 1024], P('front', 'pivot', 'rows'), may hold values from -0.1875 to 0.1875
- boundary: float32 [4, 8192, 8192], P('front', ('pivot', 'rows')), may hold values from -0.0625 to 0.0625
- rhs: float32 [4, 240, 8192], P('front', None, ('pivot', 'rows')), may hold values from -6 to 6
- boundary_rhs: float32 [4, 240, 8192], P('front', None, ('pivot', 'rows')), may hold values from -6 to 6
- owner: int32 [4, 8192, 1], P('front', ('pivot', 'rows')), may hold values from 0 to 63; in each aligned block of 128 rows (0 to 127, 128 to 255, ..., all dimensions but the last counted through in order) at most 4 rows name the same one
- slot: int32 [4, 8192], P('front', ('pivot', 'rows')), may hold values from 0 to 255
- parent_in: float32 [240, 16384], P(None, ('pivot', 'rows')), may hold values from -6 to 6
Outputs:
- solution: float32 [4, 240, 8192], P('front', None, ('pivot', 'rows'))
- parent_rhs: float32 [240, 16384], P(None, ('pivot', 'rows'))
The draws below stay inside these ranges and needn't reach their ends.
Inputs may be any that keep to these rules, and one draw needn't show every extreme that they name: Within the 128 boundary rows of one device no owner is named more than 4 times, and in every draw some device's rows name some owner exactly 4 times.
All inputs are finite; a program needn't handle non-finite values.
Results may differ from the reference program's by a relative error of at most 0.0001.
Values sent between devices are 32-bit elements; how exact they have to be, the bound alone decides.
A program may use at most 64 MiB of HBM per device.

```python
import math
import jax
import jax.numpy as jnp
import numpy as np
from jax import lax

P_SIZE = 8192
PARENT_ROWS = 16384
FRONTS = 4
NB = 8
PB = 1024
RS = 128
B = 8192
S = 240
OWNERS = 64
PROWS = 256
CAP = 4


def touch_ends(result, key, low, largest):
    extent = result.shape
    index_at = [jax.random.randint(jax.random.fold_in(key, axis), (), 0, extent[axis]) for axis in range(len(extent))]
    result = result.at[tuple(index_at)].set(low)
    longest = extent.index(max(extent))
    index_at[longest] = (index_at[longest] + 1) % extent[longest]
    return result.at[tuple(index_at)].set(largest)


def block_levels(key, extent, pieces, least, top_value):
    def one(position, blocks):
        steps = jax.random.uniform(jax.random.fold_in(jax.random.fold_in(key, 6), position), (blocks,), jnp.float32, least / len(pieces), top_value / len(pieces))
        return jnp.repeat(jnp.exp(steps), extent[position] // blocks).reshape((-1,) + (1,) * (len(extent) - position - 1))

    factor_of = one(*pieces[0])
    for cut in pieces[1:]:
        factor_of = factor_of * one(*cut)
    return factor_of


def assign_block(stream_key, own, number, rows, amount, top, reach, lean):
    order = jax.random.permutation(stream_key, amount)
    crowded, ordinary = load_shares(amount, rows * top, reach, lean, True), load_shares(amount, rows * top, reach, lean, False)
    places = jnp.arange(amount)

    def named(tallies, rotation):
        used = int((tallies > 0).sum())
        fixed = max(1, used // 4)
        moved = fixed + (places - fixed + rotation * (used - fixed)) % max(1, amount - fixed)
        return jnp.zeros((amount,), jnp.int32).at[order[jnp.where(places < fixed, places, moved)]].set(jnp.asarray(tallies, jnp.int32))

    tallies = jnp.where(number % 4 == 0, named(crowded, number // 4), named(ordinary, number - number // 4 - 1))
    mixed = jax.random.permutation(jax.random.fold_in(own, 3), amount)
    donor, taker = mixed[0:amount // 2 * 2:2], mixed[1:amount // 2 * 2:2]
    margin = jnp.minimum(tallies[donor] - 1, reach - tallies[taker]) // 2
    margin = jnp.where((donor == order[0]) | (taker == order[0]) | (tallies[taker] == 0), 0, jnp.maximum(margin, 0))
    moved = jax.random.randint(jax.random.fold_in(own, 4), (amount // 2,), 0, 1 << 20) % (margin + 1)
    tallies = tallies.at[donor].add(-moved).at[taker].add(moved)
    labels = jnp.searchsorted(jnp.cumsum(tallies), jnp.arange(rows * top), side="right").astype(jnp.int32)
    table = labels.reshape(top, rows).T
    table = table[jax.random.permutation(jax.random.fold_in(own, 1), rows)]
    rotation = jax.random.randint(jax.random.fold_in(own, 2), (rows, 1), 0, top)
    return jnp.take_along_axis(table, (jnp.arange(top)[None, :] + rotation) % top, axis=1)


def load_shares(count, total, most, skew, full):
    weights = [(1 << 20) // math.isqrt(grade ** skew) + 1 for grade in range(1, count + 1)]
    largest = most if full else min(most, max(-(-total // count), total * weights[0] // sum(weights)))
    least = 1 if total - largest >= count - 1 else 0
    counts, surplus = [largest] + [least] * (count - 1), total - largest - least * (count - 1)
    while surplus > 0:
        candidates = [i for i in range(1, count) if counts[i] < largest] or [i for i in range(1, count) if counts[i] < most]
        whole, budget = sum([weights[i] for i in candidates]), surplus
        for i in candidates:
            extra = min(most - counts[i], max(1, budget * weights[i] // whole), surplus)
            counts[i] = counts[i] + extra
            surplus = surplus - extra
    return np.array(counts)


def gaussian(key, dims, spread, most, cuts=(), dtype=jnp.bfloat16):
    values = jax.random.normal(key, dims, jnp.float32) * spread
    if len(cuts) > 0:
        values = block_levels(key, dims, cuts, -0.22, 0.18) * values
    return jnp.clip(values, min=-most, max=most).astype(dtype)


def setup_inputs(seed: int = 0) -> dict:
    key_of = jax.random.split(jax.random.key(seed), 9)
    factor = gaussian(key_of[0], (FRONTS, NB, PB, P_SIZE), P_SIZE ** -0.5, 0.0625, ((0, 4), (1, 8), (2, 8)), jnp.float32)
    inv_diag = gaussian(key_of[1], (FRONTS, NB, PB, PB), PB ** -0.5, 0.1875, ((0, 4), (1, 8), (2, 8)), jnp.float32)
    boundary = gaussian(key_of[2], (FRONTS, B, P_SIZE), P_SIZE ** -0.5, 0.0625, ((0, 4), (1, 64)), jnp.float32)
    rhs = gaussian(key_of[3], (FRONTS, S, P_SIZE), 1.0, 6.0, ((0, 4), (2, 64)), jnp.float32)
    boundary_rhs = gaussian(key_of[4], (FRONTS, S, B), 1.0, 6.0, ((0, 4), (2, 64)), jnp.float32)
    owner_keys = jax.random.split(jax.random.fold_in(key_of[5], 1), FRONTS * B // RS)
    owner_turns = jax.random.permutation(jax.random.fold_in(key_of[5], 3), FRONTS * B // RS)
    owner = jax.vmap(lambda own, number: assign_block(jax.random.fold_in(key_of[5], 2), own, number, RS, OWNERS, 1, CAP, 2))(owner_keys, owner_turns).reshape((FRONTS, B, 1))
    slot = touch_ends(jax.random.randint(key_of[6], (FRONTS, B), 0, PROWS), jax.random.fold_in(key_of[6], 1), 0, PROWS - 1).astype(jnp.int32)
    parent_in = gaussian(key_of[7], (S, PARENT_ROWS), 1.0, 6.0, ((1, 64),), jnp.float32)
    return dict(factor=factor, inv_diag=inv_diag, boundary=boundary, rhs=rhs, boundary_rhs=boundary_rhs, owner=owner, slot=slot, parent_in=parent_in)


highest = lax.Precision.HIGHEST


def reference(factor, inv_diag, boundary, rhs, boundary_rhs, owner, slot, parent_in):
    parent = parent_in
    solutions = []
    for front_idx in range(FRONTS):
        solved = jnp.zeros((S, P_SIZE), jnp.float32)
        for block_idx in range(NB):
            running = jnp.dot(solved, factor[front_idx, block_idx].T, precision=highest, preferred_element_type=jnp.float32)
            residual = rhs[front_idx][:, block_idx * PB:(block_idx + 1) * PB] - running
            block_sol = jnp.dot(residual, inv_diag[front_idx, block_idx], precision=highest, preferred_element_type=jnp.float32)
            solved = solved.at[:, block_idx * PB:(block_idx + 1) * PB].set(block_sol)
        update = boundary_rhs[front_idx] - jnp.dot(solved, boundary[front_idx].T, precision=highest, preferred_element_type=jnp.float32)
        columns = (owner[front_idx, :, 0] * PROWS + slot[front_idx]).astype(jnp.int32)
        parent = parent.at[:, columns].add(update)
        solutions.append(solved)
    return jnp.stack(solutions), parent
```

```python
import functools

import jax
import jax.numpy as jnp
from jax import lax
from jax.experimental import pallas as pl
from jax.experimental.pallas import tpu as pltpu
from jax.sharding import PartitionSpec as P

MESH = pl.DeviceIdType.MESH
F32, BF16 = jnp.float32, jnp.bfloat16
NT = (((1,), (1,)), ((), ()))
NN = (((1,), (0,)), ((), ()))
NP, NR, W = 8, 8, 128
CAP = 4


def halves(x):
    hi = x.astype(BF16)
    return hi, (x - hi.astype(F32)).astype(BF16)


def mul(a, b, dims):
    return lax.dot_general(a, b, dims, preferred_element_type=F32)


def arrived(ref, sem):
    pltpu.make_async_copy(ref, ref, sem).wait()


def kernel(
    chunks, fronts, fac, bnd, inv, rhs, brhs, own, slot, par, out_sol, out_par,
    stage, wh, wl, inv_cols, inv_hl, gath, solved, mine, acc, tosend, got, part, quarters, summed,
    load_sem, inv_s, inv_r, g1_s, g1_r, st_s, ag_s, ag_r, fw_s, fw_r, own_s, own_r,
    rs_s, rs_r, fa_s, fa_r,
):
    f, p, z = lax.axis_index("front"), lax.axis_index("pivot"), lax.axis_index("rows")
    me = p * NR + z
    core = lax.rem(p, 2)
    col = p // 2
    span = NR * W
    peers = NP * NR

    def at_z(d):
        return lax.rem(z + d + NR, NR)

    def lanes(i):
        return pl.ds(pl.multiple_of(i * W, W), W)

    def remote(src, dst, ssem, rsem, dev):
        return pltpu.make_async_remote_copy(
            src_ref=src, dst_ref=dst, send_sem=ssem, recv_sem=rsem, device_id=dev, device_id_type=MESH
        )

    load_f = pltpu.make_async_copy(fac, stage.at[pl.ds(0, W)], load_sem.at[0])
    load_b = pltpu.make_async_copy(bnd, stage.at[pl.ds(W, W)], load_sem.at[1])
    load_i = pltpu.make_async_copy(inv.at[:, lanes(z)], inv_cols.at[lanes(z), :], load_sem.at[2])
    load_f.start()
    load_b.start()
    load_i.start()

    barrier = pltpu.get_barrier_semaphore()

    @pl.loop(1, peers)
    def _(i):
        t = lax.rem(me + i, peers)
        pl.semaphore_signal(barrier, inc=1, device_id=(f, t // NR, lax.rem(t, NR)), device_id_type=MESH)

    for i in range(1, fronts):
        pl.semaphore_signal(barrier, inc=1, device_id=(lax.rem(f + i, fronts), p, z), device_id_type=MESH)
    pl.semaphore_wait(barrier, peers + fronts - 2)

    def spread(buf, rows, ssem, rsem):
        for j, d in ((2, 2), (3, -2), (0, 1), (1, -1)):
            piece = buf.at[rows, lanes(z)]
            remote(piece, piece, ssem.at[j], rsem.at[j], (f, p, at_z(d))).start()

    def part_of(rows, second):
        n = rows.size // 2
        return pl.ds(rows.start + (n if second else 0), n)

    def relay(buf, rows, ssem, rsem):
        for j, d in ((2, 1), (3, -1)):
            src = lanes(at_z(-2 * d))
            piece = buf.at[rows, src]
            arrived(piece, rsem.at[j])
            remote(piece, piece, ssem.at[j + 2], rsem.at[j + 2], (f, p, at_z(d))).start()
            some = buf.at[part_of(rows, d < 0), src]
            remote(some, some, ssem.at[j + 4], rsem.at[j + 4], (f, p, at_z(2 * d))).start()

    def finish(buf, rows, rsem):
        for j, d in ((0, -1), (1, 1), (4, -3), (5, 3)):
            arrived(buf.at[rows, lanes(at_z(d))], rsem.at[j])
        far = lanes(at_z(4))
        arrived(buf.at[part_of(rows, False), far], rsem.at[6])
        arrived(buf.at[part_of(rows, True), far], rsem.at[7])

    def sent(buf, rows, ssem):
        for j in range(6):
            arrived(buf.at[rows, lanes(z)], ssem.at[j])
        for j in (6, 7):
            arrived(buf.at[part_of(rows, False), lanes(z)], ssem.at[j])

    def start_block(c, rows):
        base = rhs[rows, :] - acc[rows, pl.ds(0, W)]
        gath[rows, lanes(z)] = base
        spread(gath, rows, g1_s.at[c], g1_r.at[c])

    acc[...] = jnp.zeros_like(acc)

    @pl.when(p == 0)
    def _():
        for c, rows in enumerate(chunks):
            start_block(c, rows)

    for d in range(1, NR):
        remote(
            inv.at[:, lanes(at_z(d))], inv_cols.at[lanes(z), :], inv_s.at[d - 1], inv_r.at[d - 1], (f, p, at_z(d))
        ).start()

    load_f.wait()
    load_b.wait()

    @pl.loop(0, NP)
    def _(k):
        cols = pl.ds(pl.multiple_of(k * span, span), span)
        hi, lo = halves(stage[:, cols])
        wh[:, cols] = hi
        wl[:, cols] = lo

    load_i.wait()
    for d in range(1, NR):
        arrived(inv_cols.at[lanes(at_z(-d)), :], inv_r.at[d - 1])
    hi, lo = halves(inv_cols[...])
    inv_hl[:, pl.ds(0, W)] = hi
    inv_hl[:, pl.ds(W, W)] = lo

    @pl.loop(0, NP)
    def _(k):
        lead = 1 - lax.rem(k, 2)
        block = solved.at[k]

        @pl.when(p == k)
        def _():
            for c, rows in enumerate(chunks):
                relay(gath, rows, g1_s.at[c], g1_r.at[c])
            for c, rows in enumerate(chunks):
                finish(gath, rows, g1_r.at[c])
                hi, lo = halves(gath[rows, :])
                both = mul(hi, inv_hl[...], NN)
                mine[rows, :] = both[:, :W] + both[:, W:] + mul(lo, inv_hl[:, pl.ds(0, W)], NN)
                for i in range(NP // 2):
                    to = lax.rem(col + i + (k % 2), NP // 2)
                    remote(
                        mine.at[rows, :], block.at[rows, lanes(z)], st_s.at[c, i], ag_r.at[k, c, 8],
                        (f, to * 2 + lead, z),
                    ).start()

        @pl.when(core == lead)
        def _():
            for c, rows in enumerate(chunks):
                arrived(block.at[rows, lanes(z)], ag_r.at[k, c, 8])
                spread(block, rows, ag_s.at[c], ag_r.at[k, c])
            for c, rows in enumerate(chunks):
                relay(block, rows, ag_s.at[c], ag_r.at[k, c])

        for c, rows in enumerate(chunks):

            @pl.when(core == lead)
            def _():
                finish(block, rows, ag_r.at[k, c])
                remote(
                    block.at[rows, :], block.at[rows, :], fw_s.at[c], fw_r.at[k, c],
                    (f, col * 2 + 1 - lead, z),
                ).start()

            @pl.when(core != lead)
            def _():
                arrived(block.at[rows, :], fw_r.at[k, c])

            cols = pl.ds(pl.multiple_of(k * span, span), span)
            hi, lo = halves(block[rows, :])
            acc[rows, :] += mul(hi, wh[:, cols], NT) + mul(lo, wh[:, cols], NT) + mul(hi, wl[:, cols], NT)

            @pl.when(p == k + 1)
            def _():
                start_block(c, rows)

        @pl.when((core != lead) & (k > 0))
        def _():
            for c, rows in enumerate(chunks):
                sent(block, rows, ag_s.at[c])
                arrived(block.at[rows, :], fw_s.at[c])

    half = mine.shape[0] // 2
    owner_col = jnp.broadcast_to(own[...], (W, W)).astype(F32)
    owner_row = owner_col.T
    first = lax.broadcasted_iota(jnp.int32, (W, W), 0)
    second = lax.broadcasted_iota(jnp.int32, (W, W), 1)
    earlier = jnp.where((owner_col == owner_row) & (first < second), 1.0, 0.0)
    position = jnp.sum(earlier, axis=0, keepdims=True)
    tile = owner_row[0:1, :] * (2 * CAP) + position
    row_id = lax.broadcasted_iota(jnp.int32, (peers * 2 * CAP, W), 0).astype(F32)
    pick = jnp.concatenate(
        [jnp.where(row_id == tile, 1.0, 0.0), jnp.where(row_id == tile + CAP, 1.0, 0.0)], axis=1
    ).astype(BF16)
    update = brhs[...] - acc[:, pl.ds(W, W)]
    tail = jnp.where(
        lax.broadcasted_iota(jnp.int32, (W - half, W), 0) == 0,
        jnp.broadcast_to(slot[...], (W - half, W)).astype(F32),
        0.0,
    )
    ext = jnp.concatenate(
        [
            jnp.concatenate([update[:half], tail], axis=0),
            jnp.concatenate([update[half:], tail], axis=0),
        ],
        axis=1,
    )
    hi, lo = halves(ext)
    tosend[...] = mul(pick, hi, NT) + mul(pick, lo, NT)

    def tiles(i):
        return pl.ds(pl.multiple_of(i * 2 * CAP, 2 * CAP), 2 * CAP)

    @pl.loop(1, peers)
    def _(i):
        t = lax.rem(me + i, peers)
        remote(
            tosend.at[tiles(t), :], got.at[tiles(me), :], own_s.at[i], own_r.at[i],
            (f, t // NR, lax.rem(t, NR)),
        ).start()

    got[tiles(me), :] = tosend[tiles(me), :]

    @pl.loop(1, peers)
    def _(i):
        t = lax.rem(me + peers - i, peers)
        arrived(got.at[tiles(t), :], own_r.at[i])

    flat = got[...].T
    slots = flat[half:half + 1, :]
    hits = jnp.where(
        slots == lax.broadcasted_iota(jnp.int32, (par.shape[1], peers * 2 * CAP), 0).astype(F32), 1.0, 0.0
    ).astype(BF16)
    which = lax.rem(lax.broadcasted_iota(jnp.int32, (W, peers * 2 * CAP), 1) // CAP, 2)
    both = jnp.concatenate([jnp.where(which == 0, flat, 0.0), jnp.where(which == 1, flat, 0.0)], axis=0)
    hi, lo = halves(both)
    part[...] = mul(hi, hits, NT) + mul(lo, hits, NT)

    band = 2 * W // fronts

    def bands(i):
        return pl.ds(pl.multiple_of(i * band, band), band)

    for i in range(1, fronts):
        t = lax.rem(f + i, fronts)
        remote(part.at[bands(t), :], quarters.at[i - 1], rs_s.at[i - 1], rs_r.at[i - 1], (t, p, z)).start()
    for i in range(1, fronts):
        arrived(quarters.at[i - 1], rs_r.at[i - 1])
    total = part[bands(f), :]
    for i in range(1, fronts):
        total = total + quarters[i - 1]
    for i in range(1, fronts):
        arrived(quarters.at[i - 1], rs_s.at[i - 1])
    summed[bands(f), :] = total
    for i in range(1, fronts):
        t = lax.rem(f + i, fronts)
        remote(summed.at[bands(f), :], summed.at[bands(f), :], fa_s.at[i - 1], fa_r.at[i - 1], (t, p, z)).start()
    for i in range(1, fronts):
        arrived(summed.at[bands(lax.rem(f + fronts - i, fronts)), :], fa_r.at[i - 1])
    out_par[0:half, :] = par[0:half, :] + summed[0:half, :]
    out_par[half:2 * half, :] = par[half:2 * half, :] + summed[W:W + half, :]
    out_sol[...] = mine[...]

    for d in range(1, NR):
        arrived(inv_cols.at[lanes(z), :], inv_s.at[d - 1])
    for c, rows in enumerate(chunks):
        sent(gath, rows, g1_s.at[c])
        for i in range(NP // 2):
            arrived(mine.at[rows, :], st_s.at[c, i])

    @pl.when(core == 0)
    def _():
        for c, rows in enumerate(chunks):
            sent(solved.at[0], rows, ag_s.at[c])
            arrived(solved.at[0].at[rows, :], fw_s.at[c])

    @pl.loop(1, peers)
    def _(i):
        arrived(tosend.at[tiles(0), :], own_s.at[i])

    for i in range(1, fronts):
        arrived(part.at[bands(f), :], fa_s.at[i - 1])


def shards(factor, inv_diag, boundary, rhs, boundary_rhs, owner, slot, parent_in):
    fronts = lax.axis_size("front")
    sources = rhs.shape[1]
    depth = factor.shape[3]
    span = NR * W
    rows = parent_in.shape[1]
    first = (sources // 2 + 15) // 16 * 16
    chunks = (pl.ds(0, first), pl.ds(first, sources - first))
    ns = len(chunks)
    any_spec, vmem = pl.BlockSpec(memory_space=pl.ANY), pl.BlockSpec(memory_space=pltpu.VMEM)
    dma = pltpu.SemaphoreType.DMA
    return pl.pallas_call(
        functools.partial(kernel, chunks, fronts),
        out_shape=(
            jax.ShapeDtypeStruct((sources, W), F32),
            jax.ShapeDtypeStruct((sources, rows), F32),
        ),
        in_specs=[any_spec] * 3 + [vmem] * 5,
        out_specs=(vmem, vmem),
        scratch_shapes=[
            pltpu.VMEM((2 * W, depth), F32),
            pltpu.VMEM((2 * W, depth), BF16),
            pltpu.VMEM((2 * W, depth), BF16),
            pltpu.VMEM((span, W), F32),
            pltpu.VMEM((span, 2 * W), BF16),
            pltpu.VMEM((sources, span), F32),
            pltpu.VMEM((NP, sources, span), F32),
            pltpu.VMEM((sources, W), F32),
            pltpu.VMEM((sources, 2 * W), F32),
            pltpu.VMEM((NP * NR * 2 * CAP, W), F32),
            pltpu.VMEM((NP * NR * 2 * CAP, W), F32),
            pltpu.VMEM((2 * W, rows), F32),
            pltpu.VMEM((max(1, fronts - 1), 2 * W // fronts, rows), F32),
            pltpu.VMEM((2 * W, rows), F32),
            dma((3,)),
            dma((NR - 1,)),
            dma((NR - 1,)),
            dma((ns, 8)),
            dma((ns, 8)),
            dma((ns, NP // 2)),
            dma((ns, 8)),
            dma((NP, ns, 9)),
            dma((ns,)),
            dma((NP, ns)),
            dma((NP * NR,)),
            dma((NP * NR,)),
            dma((fronts,)),
            dma((fronts,)),
            dma((fronts,)),
            dma((fronts,)),
        ],
        compiler_params=pltpu.CompilerParams(collective_id=0, has_side_effects=True, vmem_limit_bytes=60 << 20),
    )(factor[0, 0], boundary[0], inv_diag[0, 0], rhs[0], boundary_rhs[0], owner[0], slot, parent_in)


def body(*args):
    solved, parent = shards(*args)
    return solved[None], parent


def solution(mesh):
    placed = (
        P("front", "pivot", "rows", None),
        P("front", "pivot", "rows", None),
        P("front", ("pivot", "rows"), None),
        P("front", None, ("pivot", "rows")),
        P("front", None, ("pivot", "rows")),
        P("front", ("pivot", "rows"), None),
        P("front", ("pivot", "rows")),
        P(None, ("pivot", "rows")),
    )
    return jax.shard_map(
        body,
        mesh=mesh,
        in_specs=placed,
        out_specs=(P("front", None, ("pivot", "rows")), P(None, ("pivot", "rows"))),
        check_vma=False,
    )
```

```python
import functools

import jax
import jax.numpy as jnp
from jax import lax
from jax.experimental import pallas as pl
from jax.experimental.pallas import tpu as pltpu
from jax.sharding import PartitionSpec as P

MESH = pl.DeviceIdType.MESH
F32, BF16 = jnp.float32, jnp.bfloat16
NT = (((1,), (1,)), ((), ()))
NN = (((1,), (0,)), ((), ()))
NP, NR, W = 8, 8, 128
CAP = 4
FOLDS = {4: (-1, 1, 1), 6: (-1, 1, 3)}


def halves(x):
    hi = x.astype(BF16)
    return hi, (x - hi.astype(F32)).astype(BF16)


def mul(a, b, dims):
    return lax.dot_general(a, b, dims, preferred_element_type=F32)


def arrived(ref, sem):
    pltpu.make_async_copy(ref, ref, sem).wait()


def kernel(
    chunks, fronts, fac, bnd, inv, rhs, brhs, own, slot, par, out_sol, out_par,
    stage, wh, wl, inv_cols, inv_hl, low, gath, based, solved, mine, acc, tosend, got, part, quarters, summed,
    load_sem, inv_s, inv_r, low_s, low_r, g1_s, g1_r, st_s, ag_s, ag_r, fw_s, fw_r, own_s, own_r,
    rs_s, rs_r, fa_s, fa_r,
):
    f, p, z = lax.axis_index("front"), lax.axis_index("pivot"), lax.axis_index("rows")
    me = p * NR + z
    core = lax.rem(p, 2)
    col = p // 2
    span = NR * W
    peers = NP * NR
    folds = p < 0
    low_send, low_relay, low_use = -2, -2, -2
    for q, (one, two, three) in FOLDS.items():
        folds = folds | (p == q)
        low_send = jnp.where(p == q, one, low_send)
        low_relay = jnp.where(p == q, two, low_relay)
        low_use = jnp.where(p == q, three, low_use)

    def role(k):
        odd = lax.rem(k, 2)
        return 1 - odd, (odd == 0) & (col == k // 2)

    def at_z(d):
        return lax.rem(z + d + NR, NR)

    def lanes(i):
        return pl.ds(pl.multiple_of(i * W, W), W)

    def wide(k):
        return pl.ds(pl.multiple_of(k * span, span), span)

    def remote(src, dst, ssem, rsem, dev):
        return pltpu.make_async_remote_copy(
            src_ref=src, dst_ref=dst, send_sem=ssem, recv_sem=rsem, device_id=dev, device_id_type=MESH
        )

    load_f = pltpu.make_async_copy(fac, stage.at[pl.ds(0, W)], load_sem.at[0])
    load_b = pltpu.make_async_copy(bnd, stage.at[pl.ds(W, W)], load_sem.at[1])
    load_i = pltpu.make_async_copy(inv.at[:, lanes(z)], inv_cols.at[lanes(z), :], load_sem.at[2])
    load_f.start()
    load_b.start()
    load_i.start()

    barrier = pltpu.get_barrier_semaphore()

    @pl.loop(1, peers)
    def _(i):
        t = lax.rem(me + i, peers)
        pl.semaphore_signal(barrier, inc=1, device_id=(f, t // NR, lax.rem(t, NR)), device_id_type=MESH)

    for i in range(1, fronts):
        pl.semaphore_signal(barrier, inc=1, device_id=(lax.rem(f + i, fronts), p, z), device_id_type=MESH)
    pl.semaphore_wait(barrier, peers + fronts - 2)

    def by_lanes(buf, rows):
        def piece(i, half=None):
            if half is None:
                return buf.at[rows, lanes(i)]
            return buf.at[pl.ds(rows.start + half * (rows.size // 2), rows.size // 2), lanes(i)]

        return piece

    def by_rows(buf):
        def piece(i, half=None):
            if half is None:
                return buf.at[lanes(i), :]
            return buf.at[pl.ds(pl.multiple_of(i * W + half * (W // 2), W // 2), W // 2), :]

        return piece

    near = ((2, 2), (3, -2), (0, 1), (1, -1))

    def spread(piece, src, ssem, rsem):
        for j, d in near:
            remote(src, piece(z), ssem.at[j], rsem.at[j], (f, p, at_z(d))).start()

    def relay(piece, ssem, rsem):
        for j, d in ((2, 1), (3, -1)):
            origin = at_z(-2 * d)
            arrived(piece(origin), rsem.at[j])
            remote(piece(origin), piece(origin), ssem.at[j + 2], rsem.at[j + 2], (f, p, at_z(d))).start()
            some = piece(origin, j - 2)
            remote(some, some, ssem.at[j + 4], rsem.at[j + 4], (f, p, at_z(2 * d))).start()

    def finish(piece, rsem):
        for j, d in ((0, -1), (1, 1), (4, -3), (5, 3)):
            arrived(piece(at_z(d)), rsem.at[j])
        for h in (0, 1):
            arrived(piece(at_z(4), h), rsem.at[6 + h])

    def sent_near(piece, ssem):
        for j in range(4):
            arrived(piece(z), ssem.at[j])

    def sent_far(piece, ssem):
        for j in (4, 5):
            arrived(piece(z), ssem.at[j])
        for h in (0, 1):
            arrived(piece(z, h), ssem.at[6 + h])

    def start_block(c, rows):
        gath[rows, lanes(z)] = rhs[rows, :] - acc[rows, pl.ds(0, W)]
        piece = by_lanes(gath, rows)
        spread(piece, piece(z), g1_s.at[c], g1_r.at[c])

    def gathered(c, rows):
        finish(by_lanes(gath, rows), g1_r.at[c])
        hi, lo = halves(gath[rows, :])
        both = mul(hi, inv_hl[...], NN)
        return both[:, :W] + both[:, W:] + mul(lo, inv_hl[:, pl.ds(0, W)], NN)

    def send_solved(k, c, rows):
        target = lax.rem(k + 1, NP)
        odd = lax.rem(k, 2)
        src, dst = mine.at[rows, :], solved.at[k].at[rows, lanes(z)]

        def to(n, j, pivot, d):
            remote(src, dst, st_s.at[c, n], ag_r.at[k, c, j], (f, lax.rem(pivot, NP), at_z(d))).start()

        @pl.when(odd == 0)
        def _():
            for j, d in near:
                to(j, j, target, d)

        for i in range(NP // 2):
            to(4 + i, 8, target + 2 * i, 0)

    def send_low():
        src = fac.at[:, wide(p - 1)]
        spread(by_rows(low), src, low_s, low_r)
        pltpu.make_async_copy(src, low.at[lanes(z), :], load_sem.at[3]).start()

    def sent_block(k, when):
        lead, direct = role(k)

        @pl.when((core == lead) & when)
        def _():
            for c, rows in enumerate(chunks):
                piece = by_lanes(solved.at[0], rows)

                @pl.when(jnp.logical_not(direct))
                def _():
                    sent_near(piece, ag_s.at[lax.rem(k, 2), c])

                sent_far(piece, ag_s.at[lax.rem(k, 2), c])
                arrived(solved.at[0].at[rows, :], fw_s.at[lax.rem(k, 2), c])

    acc[...] = jnp.zeros_like(acc)

    @pl.when(p == 0)
    def _():
        for c, rows in enumerate(chunks):
            start_block(c, rows)

    def send_inv():
        for d in range(1, NR):
            remote(
                inv.at[:, lanes(at_z(d))], inv_cols.at[lanes(z), :], inv_s.at[d - 1], inv_r.at[d - 1], (f, p, at_z(d))
            ).start()

    @pl.when(core == 0)
    def _():
        send_inv()

    @pl.when(low_send == -1)
    def _():
        send_low()

    @pl.when(p == 0)
    def _():
        for c, rows in enumerate(chunks):
            relay(by_lanes(gath, rows), g1_s.at[c], g1_r.at[c])

    load_f.wait()
    load_b.wait()

    @pl.loop(0, NP)
    def _(k):
        hi, lo = halves(stage[:, wide(k)])
        wh[:, wide(k)] = hi
        wl[:, wide(k)] = lo

    @pl.when(core == 1)
    def _():
        send_inv()

    load_i.wait()
    for d in range(1, NR):
        arrived(inv_cols.at[lanes(at_z(-d)), :], inv_r.at[d - 1])
    hi, lo = halves(inv_cols[...])
    inv_hl[:, pl.ds(0, W)] = hi
    inv_hl[:, pl.ds(W, W)] = lo

    @pl.loop(0, NP)
    def _(k):
        lead, direct = role(k)
        block = solved.at[k]
        par_k = lax.rem(k, 2)

        @pl.when((p == k) & jnp.logical_not(folds))
        def _():
            @pl.when(k > 0)
            def _():
                for c, rows in enumerate(chunks):
                    relay(by_lanes(gath, rows), g1_s.at[c], g1_r.at[c])

            for c, rows in enumerate(chunks):
                mine[rows, :] = gathered(c, rows)
                send_solved(k, c, rows)

        for c, rows in enumerate(chunks):
            piece = by_lanes(block, rows)

            @pl.when((core == lead) & jnp.logical_not(direct))
            def _():
                arrived(piece(z), ag_r.at[k, c, 8])
                spread(piece, piece(z), ag_s.at[par_k, c], ag_r.at[k, c])

        for c, rows in enumerate(chunks):

            @pl.when(core == lead)
            def _():
                relay(by_lanes(block, rows), ag_s.at[par_k, c], ag_r.at[k, c])

            @pl.when((p == k + 1) & folds)
            def _():
                relay(by_lanes(gath, rows), g1_s.at[c], g1_r.at[c])

        for c, rows in enumerate(chunks):

            @pl.when((p == k + 1) & folds)
            def _():
                based[rows, :] = gathered(c, rows)

            @pl.when(core == lead)
            def _():
                piece = by_lanes(block, rows)

                @pl.when(direct)
                def _():
                    arrived(piece(z), ag_r.at[k, c, 8])

                finish(piece, ag_r.at[k, c])
                remote(
                    block.at[rows, :], block.at[rows, :], fw_s.at[par_k, c], fw_r.at[k, c], (f, col * 2 + 1 - lead, z)
                ).start()

            @pl.when(core != lead)
            def _():
                arrived(block.at[rows, :], fw_r.at[k, c])

            hi, lo = halves(block[rows, :])
            term = mul(hi, wh[:, wide(k)], NT) + mul(lo, wh[:, wide(k)], NT) + mul(hi, wl[:, wide(k)], NT)

            @pl.when((p == k + 1) & folds)
            def _():
                mine[rows, :] = based[rows, :] - term[:, :W]
                send_solved(k + 1, c, rows)

            acc[rows, :] += term

            @pl.when(jnp.where(folds, p == k + 2, p == k + 1))
            def _():
                start_block(c, rows)

        @pl.when(low_send == k)
        def _():
            send_low()

        @pl.when(low_relay == k)
        def _():
            relay(by_rows(low), low_s, low_r)

        @pl.when(low_use == k)
        def _():
            finish(by_rows(low), low_r)
            pltpu.make_async_copy(low.at[lanes(z), :], low.at[lanes(z), :], load_sem.at[3]).wait()
            ih, il = halves(inv_cols[...].T)

            @pl.loop(0, span // (2 * W))
            def _(i):
                some = pl.ds(pl.multiple_of(i * 2 * W, 2 * W), 2 * W)
                hi, lo = halves(low[:, some])
                hi, lo = halves(mul(ih, hi, NN) + mul(il, hi, NN) + mul(ih, lo, NN))
                into = pl.ds(pl.multiple_of((p - 1) * span + i * 2 * W, 2 * W), 2 * W)
                wh[pl.ds(0, W), into] = hi
                wl[pl.ds(0, W), into] = lo

        sent_block(k - 1, k > 0)

    half = mine.shape[0] // 2
    owner_col = jnp.broadcast_to(own[...], (W, W)).astype(F32)
    owner_row = owner_col.T
    first = lax.broadcasted_iota(jnp.int32, (W, W), 0)
    second = lax.broadcasted_iota(jnp.int32, (W, W), 1)
    earlier = jnp.where((owner_col == owner_row) & (first < second), 1.0, 0.0)
    position = jnp.sum(earlier, axis=0, keepdims=True)
    tile = owner_row[0:1, :] * (2 * CAP) + position
    row_id = lax.broadcasted_iota(jnp.int32, (peers * 2 * CAP, W), 0).astype(F32)
    pick = jnp.concatenate(
        [jnp.where(row_id == tile, 1.0, 0.0), jnp.where(row_id == tile + CAP, 1.0, 0.0)], axis=1
    ).astype(BF16)
    update = brhs[...] - acc[:, pl.ds(W, W)]
    tail = jnp.where(
        lax.broadcasted_iota(jnp.int32, (W - half, W), 0) == 0,
        jnp.broadcast_to(slot[...], (W - half, W)).astype(F32),
        0.0,
    )
    ext = jnp.concatenate(
        [
            jnp.concatenate([update[:half], tail], axis=0),
            jnp.concatenate([update[half:], tail], axis=0),
        ],
        axis=1,
    )
    hi, lo = halves(ext)
    tosend[...] = mul(pick, hi, NT) + mul(pick, lo, NT)

    def tiles(i):
        return pl.ds(pl.multiple_of(i * 2 * CAP, 2 * CAP), 2 * CAP)

    @pl.loop(1, peers)
    def _(i):
        t = lax.rem(me + i, peers)
        remote(
            tosend.at[tiles(t), :], got.at[tiles(me), :], own_s.at[i], own_r.at[i],
            (f, t // NR, lax.rem(t, NR)),
        ).start()

    got[tiles(me), :] = tosend[tiles(me), :]

    @pl.loop(1, peers)
    def _(i):
        t = lax.rem(me + peers - i, peers)
        arrived(got.at[tiles(t), :], own_r.at[i])

    flat = got[...].T
    slots = flat[half:half + 1, :]
    hits = jnp.where(
        slots == lax.broadcasted_iota(jnp.int32, (par.shape[1], peers * 2 * CAP), 0).astype(F32), 1.0, 0.0
    ).astype(BF16)
    which = lax.rem(lax.broadcasted_iota(jnp.int32, (W, peers * 2 * CAP), 1) // CAP, 2)
    both = jnp.concatenate([jnp.where(which == 0, flat, 0.0), jnp.where(which == 1, flat, 0.0)], axis=0)
    hi, lo = halves(both)
    part[...] = mul(hi, hits, NT) + mul(lo, hits, NT)

    band = 2 * W // fronts

    def bands(i):
        return pl.ds(pl.multiple_of(i * band, band), band)

    for i in range(1, fronts):
        t = lax.rem(f + i, fronts)
        remote(part.at[bands(t), :], quarters.at[i - 1], rs_s.at[i - 1], rs_r.at[i - 1], (t, p, z)).start()
    for i in range(1, fronts):
        arrived(quarters.at[i - 1], rs_r.at[i - 1])
    total = part[bands(f), :]
    for i in range(1, fronts):
        total = total + quarters[i - 1]
    for i in range(1, fronts):
        arrived(quarters.at[i - 1], rs_s.at[i - 1])
    summed[bands(f), :] = total
    for i in range(1, fronts):
        t = lax.rem(f + i, fronts)
        remote(summed.at[bands(f), :], summed.at[bands(f), :], fa_s.at[i - 1], fa_r.at[i - 1], (t, p, z)).start()
    for i in range(1, fronts):
        arrived(summed.at[bands(lax.rem(f + fronts - i, fronts)), :], fa_r.at[i - 1])
    out_par[0:half, :] = par[0:half, :] + summed[0:half, :]
    out_par[half:2 * half, :] = par[half:2 * half, :] + summed[W:W + half, :]
    out_sol[...] = mine[...]

    for d in range(1, NR):
        arrived(inv_cols.at[lanes(z), :], inv_s.at[d - 1])
    for c, rows in enumerate(chunks):
        piece = by_lanes(gath, rows)
        sent_near(piece, g1_s.at[c])
        sent_far(piece, g1_s.at[c])
        for i in range(4, 8):
            arrived(mine.at[rows, :], st_s.at[c, i])

        @pl.when(core == 0)
        def _():
            for i in range(4):
                arrived(mine.at[rows, :], st_s.at[c, i])

    @pl.when(folds)
    def _():
        sent_near(by_rows(low), low_s)
        sent_far(by_rows(low), low_s)

    sent_block(jnp.int32(NP - 1), True)

    @pl.loop(1, peers)
    def _(i):
        arrived(tosend.at[tiles(0), :], own_s.at[i])

    for i in range(1, fronts):
        arrived(part.at[bands(f), :], fa_s.at[i - 1])


def shards(factor, inv_diag, boundary, rhs, boundary_rhs, owner, slot, parent_in):
    fronts = lax.axis_size("front")
    sources = rhs.shape[1]
    depth = factor.shape[3]
    span = NR * W
    rows = parent_in.shape[1]
    size = sources // 3
    chunks = tuple(pl.ds(i * size, size) for i in range(3))
    ns = len(chunks)
    any_spec, vmem = pl.BlockSpec(memory_space=pl.ANY), pl.BlockSpec(memory_space=pltpu.VMEM)
    dma = pltpu.SemaphoreType.DMA
    return pl.pallas_call(
        functools.partial(kernel, chunks, fronts),
        out_shape=(
            jax.ShapeDtypeStruct((sources, W), F32),
            jax.ShapeDtypeStruct((sources, rows), F32),
        ),
        in_specs=[any_spec] * 3 + [vmem] * 5,
        out_specs=(vmem, vmem),
        scratch_shapes=[
            pltpu.VMEM((2 * W, depth), F32),
            pltpu.VMEM((2 * W, depth), BF16),
            pltpu.VMEM((2 * W, depth), BF16),
            pltpu.VMEM((span, W), F32),
            pltpu.VMEM((span, 2 * W), BF16),
            pltpu.VMEM((span, span), F32),
            pltpu.VMEM((sources, span), F32),
            pltpu.VMEM((sources, W), F32),
            pltpu.VMEM((NP, sources, span), F32),
            pltpu.VMEM((sources, W), F32),
            pltpu.VMEM((sources, 2 * W), F32),
            pltpu.VMEM((NP * NR * 2 * CAP, W), F32),
            pltpu.VMEM((NP * NR * 2 * CAP, W), F32),
            pltpu.VMEM((2 * W, rows), F32),
            pltpu.VMEM((max(1, fronts - 1), 2 * W // fronts, rows), F32),
            pltpu.VMEM((2 * W, rows), F32),
            dma((4,)),
            dma((NR - 1,)),
            dma((NR - 1,)),
            dma((8,)),
            dma((8,)),
            dma((ns, 8)),
            dma((ns, 8)),
            dma((ns, 8)),
            dma((2, ns, 8)),
            dma((NP, ns, 9)),
            dma((2, ns)),
            dma((NP, ns)),
            dma((NP * NR,)),
            dma((NP * NR,)),
            dma((fronts,)),
            dma((fronts,)),
            dma((fronts,)),
            dma((fronts,)),
        ],
        compiler_params=pltpu.CompilerParams(collective_id=0, has_side_effects=True, vmem_limit_bytes=60 << 20),
    )(factor[0, 0], boundary[0], inv_diag[0, 0], rhs[0], boundary_rhs[0], owner[0], slot, parent_in)


def body(*args):
    solved, parent = shards(*args)
    return solved[None], parent


def solution(mesh):
    placed = (
        P("front", "pivot", "rows", None),
        P("front", "pivot", "rows", None),
        P("front", ("pivot", "rows"), None),
        P("front", None, ("pivot", "rows")),
        P("front", None, ("pivot", "rows")),
        P("front", ("pivot", "rows"), None),
        P("front", ("pivot", "rows")),
        P(None, ("pivot", "rows")),
    )
    return jax.shard_map(
        body,
        mesh=mesh,
        in_specs=placed,
        out_specs=(P("front", None, ("pivot", "rows")), P(None, ("pivot", "rows"))),
        check_vma=False,
    )
```

```python
import functools

import jax
import jax.numpy as jnp
from jax import lax
from jax.experimental import pallas as pl
from jax.experimental.pallas import tpu as pltpu
from jax.sharding import PartitionSpec as P

MESH = pl.DeviceIdType.MESH
F32, BF16 = jnp.float32, jnp.bfloat16
NT = (((1,), (1,)), ((), ()))
NN = (((1,), (0,)), ((), ()))
NP, NR, W = 8, 8, 128
CAP = 4
FOLDS = {4: (-1, 1, 1), 6: (-1, 1, 3)}


def halves(x):
    hi = x.astype(BF16)
    return hi, (x - hi.astype(F32)).astype(BF16)


def mul(a, b, dims):
    return lax.dot_general(a, b, dims, preferred_element_type=F32)


def arrived(ref, sem):
    pltpu.make_async_copy(ref, ref, sem).wait()


def kernel(
    chunks, fronts, fac, bnd, inv, rhs, brhs, own, slot, par, out_sol, out_par,
    stage, wh, wl, inv_cols, inv_hl, low, gath, based, solved, mine, acc, pick, tosend, got, part, quarters, summed,
    load_sem, inv_s, inv_r, low_s, low_r, g1_s, g1_r, st_s, ag_s, ag_r, fw_s, fw_r, own_s, own_r,
    rs_s, rs_r, fa_s, fa_r,
):
    f, p, z = lax.axis_index("front"), lax.axis_index("pivot"), lax.axis_index("rows")
    me = p * NR + z
    core = lax.rem(p, 2)
    col = p // 2
    span = NR * W
    peers = NP * NR
    folds = p < 0
    low_send, low_relay, low_use = -2, -2, -2
    for q, (one, two, three) in FOLDS.items():
        folds = folds | (p == q)
        low_send = jnp.where(p == q, one, low_send)
        low_relay = jnp.where(p == q, two, low_relay)
        low_use = jnp.where(p == q, three, low_use)

    def role(k):
        odd = lax.rem(k, 2)
        return 1 - odd, (odd == 0) & (col == k // 2)

    def at_z(d):
        return lax.rem(z + d + NR, NR)

    def lanes(i):
        return pl.ds(pl.multiple_of(i * W, W), W)

    def wide(k):
        return pl.ds(pl.multiple_of(k * span, span), span)

    def remote(src, dst, ssem, rsem, dev):
        return pltpu.make_async_remote_copy(
            src_ref=src, dst_ref=dst, send_sem=ssem, recv_sem=rsem, device_id=dev, device_id_type=MESH
        )

    load_f = pltpu.make_async_copy(fac, stage.at[pl.ds(0, W)], load_sem.at[0])
    load_b = pltpu.make_async_copy(bnd, stage.at[pl.ds(W, W)], load_sem.at[1])
    load_i = pltpu.make_async_copy(inv.at[:, lanes(z)], inv_cols.at[lanes(z), :], load_sem.at[2])
    load_f.start()
    load_b.start()
    load_i.start()

    barrier = pltpu.get_barrier_semaphore()

    @pl.loop(1, peers)
    def _(i):
        t = lax.rem(me + i, peers)
        pl.semaphore_signal(barrier, inc=1, device_id=(f, t // NR, lax.rem(t, NR)), device_id_type=MESH)

    for i in range(1, fronts):
        pl.semaphore_signal(barrier, inc=1, device_id=(lax.rem(f + i, fronts), p, z), device_id_type=MESH)
    pl.semaphore_wait(barrier, peers + fronts - 2)

    def by_lanes(buf, rows):
        def piece(i, half=None):
            if half is None:
                return buf.at[rows, lanes(i)]
            return buf.at[pl.ds(rows.start + half * (rows.size // 2), rows.size // 2), lanes(i)]

        return piece

    def by_rows(buf):
        def piece(i, half=None):
            if half is None:
                return buf.at[lanes(i), :]
            return buf.at[pl.ds(pl.multiple_of(i * W + half * (W // 2), W // 2), W // 2), :]

        return piece

    near = ((2, 2), (3, -2), (0, 1), (1, -1))

    def spread(piece, src, ssem, rsem):
        for j, d in near:
            remote(src, piece(z), ssem.at[j], rsem.at[j], (f, p, at_z(d))).start()

    def relay(piece, ssem, rsem):
        for j, d in ((2, 1), (3, -1)):
            origin = at_z(-2 * d)
            arrived(piece(origin), rsem.at[j])
            remote(piece(origin), piece(origin), ssem.at[j + 2], rsem.at[j + 2], (f, p, at_z(d))).start()
            some = piece(origin, j - 2)
            remote(some, some, ssem.at[j + 4], rsem.at[j + 4], (f, p, at_z(2 * d))).start()

    def finish(piece, rsem):
        for j, d in ((0, -1), (1, 1), (4, -3), (5, 3)):
            arrived(piece(at_z(d)), rsem.at[j])
        for h in (0, 1):
            arrived(piece(at_z(4), h), rsem.at[6 + h])

    def sent_near(piece, ssem):
        for j in range(4):
            arrived(piece(z), ssem.at[j])

    def sent_far(piece, ssem):
        for j in (4, 5):
            arrived(piece(z), ssem.at[j])
        for h in (0, 1):
            arrived(piece(z, h), ssem.at[6 + h])

    def start_block(c, rows):
        gath[rows, lanes(z)] = rhs[rows, :] - acc[rows, pl.ds(0, W)]
        piece = by_lanes(gath, rows)
        spread(piece, piece(z), g1_s.at[c], g1_r.at[c])

    def gathered(c, rows):
        finish(by_lanes(gath, rows), g1_r.at[c])
        hi, lo = halves(gath[rows, :])
        both = mul(jnp.concatenate([hi, lo], axis=0), inv_hl[...], NN)
        both = both[:, :W] + both[:, W:]
        return both[:rows.size] + both[rows.size:]

    def send_solved(k, c, rows):
        target = lax.rem(k + 1, NP)
        odd = lax.rem(k, 2)
        src, dst = mine.at[rows, :], solved.at[k].at[rows, lanes(z)]

        def to(n, j, pivot, d):
            remote(src, dst, st_s.at[c, n], ag_r.at[k, c, j], (f, lax.rem(pivot, NP), at_z(d))).start()

        @pl.when(odd == 0)
        def _():
            for j, d in near:
                to(j, j, target, d)

        for i in range(NP // 2):
            to(4 + i, 8, target + 2 * i, 0)

    def send_low():
        src = fac.at[:, wide(p - 1)]
        spread(by_rows(low), src, low_s, low_r)
        pltpu.make_async_copy(src, low.at[lanes(z), :], load_sem.at[3]).start()

    def sent_block(k, when):
        lead, direct = role(k)

        @pl.when((core == lead) & when)
        def _():
            for c, rows in enumerate(chunks):
                piece = by_lanes(solved.at[0], rows)

                @pl.when(jnp.logical_not(direct))
                def _():
                    sent_near(piece, ag_s.at[lax.rem(k, 2), c])

                sent_far(piece, ag_s.at[lax.rem(k, 2), c])
                arrived(solved.at[0].at[rows, :], fw_s.at[lax.rem(k, 2), c])

    acc[...] = jnp.zeros_like(acc)

    @pl.when(p == 0)
    def _():
        for c, rows in enumerate(chunks):
            start_block(c, rows)

    def send_inv():
        for d in range(1, NR):
            remote(
                inv.at[:, lanes(at_z(d))], inv_cols.at[lanes(z), :], inv_s.at[d - 1], inv_r.at[d - 1], (f, p, at_z(d))
            ).start()

    @pl.when(core == 0)
    def _():
        send_inv()

    @pl.when(low_send == -1)
    def _():
        send_low()

    @pl.when(p == 0)
    def _():
        for c, rows in enumerate(chunks):
            relay(by_lanes(gath, rows), g1_s.at[c], g1_r.at[c])

    load_f.wait()
    load_b.wait()

    @pl.loop(0, NP)
    def _(k):
        hi, lo = halves(stage[:, wide(k)])
        wh[:, wide(k)] = hi
        wl[:, wide(k)] = lo

    @pl.when(core == 1)
    def _():
        send_inv()

    owner_row = jnp.broadcast_to(own[...], (W, W)).astype(F32)
    owner_col = owner_row.T
    first = lax.broadcasted_iota(jnp.int32, (W, W), 0)
    second = lax.broadcasted_iota(jnp.int32, (W, W), 1)
    earlier = jnp.where((owner_col == owner_row) & (first < second), 1.0, 0.0)
    position = jnp.sum(earlier, axis=0, keepdims=True)
    tile = owner_row[0:1, :] * (2 * CAP) + position
    row_id = lax.broadcasted_iota(jnp.int32, (peers * 2 * CAP, W), 0).astype(F32)
    pick[...] = jnp.concatenate(
        [jnp.where(row_id == tile, 1.0, 0.0), jnp.where(row_id == tile + CAP, 1.0, 0.0)], axis=1
    ).astype(BF16)

    load_i.wait()
    for d in range(1, NR):
        arrived(inv_cols.at[lanes(at_z(-d)), :], inv_r.at[d - 1])
    hi, lo = halves(inv_cols[...])
    inv_hl[:, pl.ds(0, W)] = hi
    inv_hl[:, pl.ds(W, W)] = lo

    @pl.loop(0, NP)
    def _(k):
        lead, direct = role(k)
        block = solved.at[k]
        par_k = lax.rem(k, 2)

        @pl.when((p == k) & jnp.logical_not(folds))
        def _():
            @pl.when(k > 0)
            def _():
                for c, rows in enumerate(chunks):
                    relay(by_lanes(gath, rows), g1_s.at[c], g1_r.at[c])

            for c, rows in enumerate(chunks):
                mine[rows, :] = gathered(c, rows)
                send_solved(k, c, rows)

        for c, rows in enumerate(chunks):
            piece = by_lanes(block, rows)

            @pl.when((core == lead) & jnp.logical_not(direct))
            def _():
                arrived(piece(z), ag_r.at[k, c, 8])
                spread(piece, piece(z), ag_s.at[par_k, c], ag_r.at[k, c])

        for c, rows in enumerate(chunks):

            @pl.when(core == lead)
            def _():
                relay(by_lanes(block, rows), ag_s.at[par_k, c], ag_r.at[k, c])

            @pl.when((p == k + 1) & folds)
            def _():
                relay(by_lanes(gath, rows), g1_s.at[c], g1_r.at[c])

        for c, rows in enumerate(chunks):

            @pl.when((p == k + 1) & folds)
            def _():
                based[rows, :] = gathered(c, rows)

            @pl.when(core == lead)
            def _():
                piece = by_lanes(block, rows)

                @pl.when(direct)
                def _():
                    arrived(piece(z), ag_r.at[k, c, 8])

                finish(piece, ag_r.at[k, c])
                remote(
                    block.at[rows, :], block.at[rows, :], fw_s.at[par_k, c], fw_r.at[k, c], (f, col * 2 + 1 - lead, z)
                ).start()

            @pl.when(core != lead)
            def _():
                arrived(block.at[rows, :], fw_r.at[k, c])

            hi, lo = halves(block[rows, :])
            both = mul(jnp.concatenate([hi, lo], axis=0), wh[:, wide(k)], NT)
            term = both[:rows.size] + both[rows.size:] + mul(hi, wl[:, wide(k)], NT)

            @pl.when((p == k + 1) & folds)
            def _():
                mine[rows, :] = based[rows, :] - term[:, :W]
                send_solved(k + 1, c, rows)

            acc[rows, :] += term

            @pl.when(jnp.where(folds, p == k + 2, p == k + 1))
            def _():
                start_block(c, rows)

        @pl.when(low_send == k)
        def _():
            send_low()

        @pl.when(low_relay == k)
        def _():
            relay(by_rows(low), low_s, low_r)

        @pl.when(low_use == k)
        def _():
            finish(by_rows(low), low_r)
            pltpu.make_async_copy(low.at[lanes(z), :], low.at[lanes(z), :], load_sem.at[3]).wait()
            ih, il = halves(inv_cols[...].T)

            @pl.loop(0, span // (2 * W))
            def _(i):
                some = pl.ds(pl.multiple_of(i * 2 * W, 2 * W), 2 * W)
                hi, lo = halves(low[:, some])
                hi, lo = halves(mul(ih, hi, NN) + mul(il, hi, NN) + mul(ih, lo, NN))
                into = pl.ds(pl.multiple_of((p - 1) * span + i * 2 * W, 2 * W), 2 * W)
                wh[pl.ds(0, W), into] = hi
                wl[pl.ds(0, W), into] = lo

        sent_block(k - 1, k > 0)

    half = mine.shape[0] // 2
    update = brhs[...] - acc[:, pl.ds(W, W)]
    tail = jnp.where(
        lax.broadcasted_iota(jnp.int32, (W - half, W), 0) == 0,
        jnp.broadcast_to(slot[...], (W - half, W)).astype(F32),
        0.0,
    )
    ext = jnp.concatenate(
        [
            jnp.concatenate([update[:half], tail], axis=0),
            jnp.concatenate([update[half:], tail], axis=0),
        ],
        axis=1,
    )
    hi, lo = halves(ext)
    tosend[...] = mul(pick[...], hi, NT) + mul(pick[...], lo, NT)

    def tiles(i):
        return pl.ds(pl.multiple_of(i * 2 * CAP, 2 * CAP), 2 * CAP)

    @pl.loop(1, peers)
    def _(i):
        t = lax.rem(me + i, peers)
        remote(
            tosend.at[tiles(t), :], got.at[tiles(me), :], own_s.at[i], own_r.at[i],
            (f, t // NR, lax.rem(t, NR)),
        ).start()

    got[tiles(me), :] = tosend[tiles(me), :]

    for d in range(1, NR):
        arrived(inv_cols.at[lanes(z), :], inv_s.at[d - 1])
    for c, rows in enumerate(chunks):
        piece = by_lanes(gath, rows)
        sent_near(piece, g1_s.at[c])
        sent_far(piece, g1_s.at[c])
        for i in range(4, 8):
            arrived(mine.at[rows, :], st_s.at[c, i])

        @pl.when(core == 0)
        def _():
            for i in range(4):
                arrived(mine.at[rows, :], st_s.at[c, i])

    @pl.when(folds)
    def _():
        sent_near(by_rows(low), low_s)
        sent_far(by_rows(low), low_s)

    sent_block(jnp.int32(NP - 1), True)

    @pl.loop(1, peers)
    def _(i):
        t = lax.rem(me + peers - i, peers)
        arrived(got.at[tiles(t), :], own_r.at[i])

    flat = got[...].T
    slots = flat[half:half + 1, :]
    hits = jnp.where(
        slots == lax.broadcasted_iota(jnp.int32, (par.shape[1], peers * 2 * CAP), 0).astype(F32), 1.0, 0.0
    ).astype(BF16)
    which = lax.rem(lax.broadcasted_iota(jnp.int32, (W, peers * 2 * CAP), 1) // CAP, 2)
    both = jnp.concatenate([jnp.where(which == 0, flat, 0.0), jnp.where(which == 1, flat, 0.0)], axis=0)
    hi, lo = halves(both)
    part[...] = mul(hi, hits, NT) + mul(lo, hits, NT)

    band = 2 * W // fronts

    def bands(i):
        return pl.ds(pl.multiple_of(i * band, band), band)

    for i in range(1, fronts):
        t = lax.rem(f + i, fronts)
        remote(part.at[bands(t), :], quarters.at[i - 1], rs_s.at[i - 1], rs_r.at[i - 1], (t, p, z)).start()
    @pl.loop(1, peers)
    def _(i):
        arrived(tosend.at[tiles(0), :], own_s.at[i])

    for i in range(1, fronts):
        arrived(quarters.at[i - 1], rs_r.at[i - 1])
    total = part[bands(f), :]
    for i in range(1, fronts):
        total = total + quarters[i - 1]
    summed[bands(f), :] = total
    for i in range(1, fronts):
        t = lax.rem(f + i, fronts)
        remote(summed.at[bands(f), :], summed.at[bands(f), :], fa_s.at[i - 1], fa_r.at[i - 1], (t, p, z)).start()
    out_sol[...] = mine[...]
    for i in range(1, fronts):
        arrived(quarters.at[i - 1], rs_s.at[i - 1])
    for i in range(1, fronts):
        arrived(summed.at[bands(lax.rem(f + fronts - i, fronts)), :], fa_r.at[i - 1])
    out_par[0:half, :] = par[0:half, :] + summed[0:half, :]
    out_par[half:2 * half, :] = par[half:2 * half, :] + summed[W:W + half, :]
    for i in range(1, fronts):
        arrived(part.at[bands(f), :], fa_s.at[i - 1])


def shards(factor, inv_diag, boundary, rhs, boundary_rhs, owner, slot, parent_in):
    fronts = lax.axis_size("front")
    sources = rhs.shape[1]
    depth = factor.shape[3]
    span = NR * W
    rows = parent_in.shape[1]
    size = (sources // 4 + 15) // 16 * 16
    chunks = tuple(pl.ds(i, min(size, sources - i)) for i in range(0, sources, size))
    ns = len(chunks)
    any_spec, vmem = pl.BlockSpec(memory_space=pl.ANY), pl.BlockSpec(memory_space=pltpu.VMEM)
    dma = pltpu.SemaphoreType.DMA
    return pl.pallas_call(
        functools.partial(kernel, chunks, fronts),
        out_shape=(
            jax.ShapeDtypeStruct((sources, W), F32),
            jax.ShapeDtypeStruct((sources, rows), F32),
        ),
        in_specs=[any_spec] * 3 + [vmem] * 5,
        out_specs=(vmem, vmem),
        scratch_shapes=[
            pltpu.VMEM((2 * W, depth), F32),
            pltpu.VMEM((2 * W, depth), BF16),
            pltpu.VMEM((2 * W, depth), BF16),
            pltpu.VMEM((span, W), F32),
            pltpu.VMEM((span, 2 * W), BF16),
            pltpu.VMEM((span, span), F32),
            pltpu.VMEM((sources, span), F32),
            pltpu.VMEM((sources, W), F32),
            pltpu.VMEM((NP, sources, span), F32),
            pltpu.VMEM((sources, W), F32),
            pltpu.VMEM((sources, 2 * W), F32),
            pltpu.VMEM((NP * NR * 2 * CAP, 2 * W), BF16),
            pltpu.VMEM((NP * NR * 2 * CAP, W), F32),
            pltpu.VMEM((NP * NR * 2 * CAP, W), F32),
            pltpu.VMEM((2 * W, rows), F32),
            pltpu.VMEM((max(1, fronts - 1), 2 * W // fronts, rows), F32),
            pltpu.VMEM((2 * W, rows), F32),
            dma((4,)),
            dma((NR - 1,)),
            dma((NR - 1,)),
            dma((8,)),
            dma((8,)),
            dma((ns, 8)),
            dma((ns, 8)),
            dma((ns, 8)),
            dma((2, ns, 8)),
            dma((NP, ns, 9)),
            dma((2, ns)),
            dma((NP, ns)),
            dma((NP * NR,)),
            dma((NP * NR,)),
            dma((fronts,)),
            dma((fronts,)),
            dma((fronts,)),
            dma((fronts,)),
        ],
        compiler_params=pltpu.CompilerParams(collective_id=0, has_side_effects=True, vmem_limit_bytes=60 << 20),
    )(factor[0, 0], boundary[0], inv_diag[0, 0], rhs[0], boundary_rhs[0], owner[:, :, 0], slot, parent_in)


def body(*args):
    solved, parent = shards(*args)
    return solved[None], parent


def solution(mesh):
    placed = (
        P("front", "pivot", "rows", None),
        P("front", "pivot", "rows", None),
        P("front", ("pivot", "rows"), None),
        P("front", None, ("pivot", "rows")),
        P("front", None, ("pivot", "rows")),
        P("front", ("pivot", "rows"), None),
        P("front", ("pivot", "rows")),
        P(None, ("pivot", "rows")),
    )
    return jax.shard_map(
        body,
        mesh=mesh,
        in_specs=placed,
        out_specs=(P("front", None, ("pivot", "rows")), P(None, ("pivot", "rows"))),
        check_vma=False,
    )
```

```python
import functools

import jax
import jax.numpy as jnp
from jax import lax
from jax.experimental import pallas as pl
from jax.experimental.pallas import tpu as pltpu
from jax.sharding import PartitionSpec as P

MESH = pl.DeviceIdType.MESH
F32, BF16 = jnp.float32, jnp.bfloat16
NT = (((1,), (1,)), ((), ()))
NN = (((1,), (0,)), ((), ()))
NP, NR, W = 8, 8, 128
CAP = 4
FOLDS = {4: (-1, 1, 1), 6: (-1, 1, 2)}


def halves(x):
    hi = x.astype(BF16)
    return hi, (x - hi.astype(F32)).astype(BF16)


def mul(a, b, dims):
    return lax.dot_general(a, b, dims, preferred_element_type=F32)


def arrived(ref, sem):
    pltpu.make_async_copy(ref, ref, sem).wait()


def kernel(
    chunks, fronts, fac, bnd, inv, rhs, brhs, own, slot, par, out_sol, out_par,
    stage, wh, wl, inv_cols, inv_hl, low, gath, based, solved, mine, acc, pick, tosend, got, part, quarters, summed,
    load_sem, inv_s, inv_r, low_s, low_r, g1_s, g1_r, st_s, ag_s, ag_r, fw_s, fw_r, own_s, own_r,
    rs_s, rs_r, fa_s, fa_r,
):
    f, p, z = lax.axis_index("front"), lax.axis_index("pivot"), lax.axis_index("rows")
    me = p * NR + z
    core = lax.rem(p, 2)
    col = p // 2
    span = NR * W
    peers = NP * NR
    folds = p < 0
    low_send, low_relay, low_use = -2, -2, -2
    for q, (one, two, three) in FOLDS.items():
        folds = folds | (p == q)
        low_send = jnp.where(p == q, one, low_send)
        low_relay = jnp.where(p == q, two, low_relay)
        low_use = jnp.where(p == q, three, low_use)

    def role(k):
        odd = lax.rem(k, 2)
        return 1 - odd, (odd == 0) & (col == k // 2)

    def at_z(d):
        return lax.rem(z + d + NR, NR)

    def lanes(i):
        return pl.ds(pl.multiple_of(i * W, W), W)

    def wide(k):
        return pl.ds(pl.multiple_of(k * span, span), span)

    def remote(src, dst, ssem, rsem, dev):
        return pltpu.make_async_remote_copy(
            src_ref=src, dst_ref=dst, send_sem=ssem, recv_sem=rsem, device_id=dev, device_id_type=MESH
        )

    load_f = pltpu.make_async_copy(fac, stage.at[pl.ds(0, W)], load_sem.at[0])
    load_b = pltpu.make_async_copy(bnd, stage.at[pl.ds(W, W)], load_sem.at[1])
    load_i = pltpu.make_async_copy(inv.at[:, lanes(z)], inv_cols.at[lanes(z), :], load_sem.at[2])
    load_f.start()
    load_b.start()
    load_i.start()

    barrier = pltpu.get_barrier_semaphore()

    @pl.loop(1, peers)
    def _(i):
        t = lax.rem(me + i, peers)
        pl.semaphore_signal(barrier, inc=1, device_id=(f, t // NR, lax.rem(t, NR)), device_id_type=MESH)

    for i in range(1, fronts):
        pl.semaphore_signal(barrier, inc=1, device_id=(lax.rem(f + i, fronts), p, z), device_id_type=MESH)
    pl.semaphore_wait(barrier, peers + fronts - 2)

    def by_lanes(buf, rows):
        def piece(i, half=None):
            if half is None:
                return buf.at[rows, lanes(i)]
            return buf.at[pl.ds(rows.start + half * (rows.size // 2), rows.size // 2), lanes(i)]

        return piece

    def by_rows(buf):
        def piece(i, half=None):
            if half is None:
                return buf.at[lanes(i), :]
            return buf.at[pl.ds(pl.multiple_of(i * W + half * (W // 2), W // 2), W // 2), :]

        return piece

    near = ((2, 2), (3, -2), (0, 1), (1, -1))

    def spread(piece, src, ssem, rsem):
        for j, d in near:
            remote(src, piece(z), ssem.at[j], rsem.at[j], (f, p, at_z(d))).start()

    def relay(piece, ssem, rsem):
        for j, d in ((2, 1), (3, -1)):
            origin = at_z(-2 * d)
            arrived(piece(origin), rsem.at[j])
            remote(piece(origin), piece(origin), ssem.at[j + 2], rsem.at[j + 2], (f, p, at_z(d))).start()
            some = piece(origin, j - 2)
            remote(some, some, ssem.at[j + 4], rsem.at[j + 4], (f, p, at_z(2 * d))).start()

    def finish(piece, rsem):
        for j, d in ((0, -1), (1, 1), (4, -3), (5, 3)):
            arrived(piece(at_z(d)), rsem.at[j])
        for h in (0, 1):
            arrived(piece(at_z(4), h), rsem.at[6 + h])

    def sent_near(piece, ssem):
        for j in range(4):
            arrived(piece(z), ssem.at[j])

    def sent_far(piece, ssem):
        for j in (4, 5):
            arrived(piece(z), ssem.at[j])
        for h in (0, 1):
            arrived(piece(z, h), ssem.at[6 + h])

    def start_block(c, rows):
        gath[rows, lanes(z)] = rhs[rows, :] - acc[rows, pl.ds(0, W)]
        piece = by_lanes(gath, rows)
        spread(piece, piece(z), g1_s.at[c], g1_r.at[c])

    def gathered(c, rows):
        finish(by_lanes(gath, rows), g1_r.at[c])
        hi, lo = halves(gath[rows, :])
        both = mul(jnp.concatenate([hi, lo], axis=0), inv_hl[...], NN)
        both = both[:, :W] + both[:, W:]
        return both[:rows.size] + both[rows.size:]

    def send_solved(k, c, rows):
        target = lax.rem(k + 1, NP)
        odd = lax.rem(k, 2)
        src, dst = mine.at[rows, :], solved.at[k].at[rows, lanes(z)]

        def to(n, j, pivot, d):
            remote(src, dst, st_s.at[c, n], ag_r.at[k, c, j], (f, lax.rem(pivot, NP), at_z(d))).start()

        @pl.when(odd == 0)
        def _():
            for j, d in near:
                to(j, j, target, d)

        for i in range(NP // 2):
            to(4 + i, 8, target + 2 * i, 0)

    def send_low():
        src = fac.at[:, wide(p - 1)]
        spread(by_rows(low), src, low_s, low_r)
        pltpu.make_async_copy(src, low.at[lanes(z), :], load_sem.at[3]).start()

    def sent_block(k, when):
        lead, direct = role(k)

        @pl.when((core == lead) & when)
        def _():
            for c, rows in enumerate(chunks):
                piece = by_lanes(solved.at[0], rows)

                @pl.when(jnp.logical_not(direct))
                def _():
                    sent_near(piece, ag_s.at[lax.rem(k, 2), c])

                sent_far(piece, ag_s.at[lax.rem(k, 2), c])
                arrived(solved.at[0].at[rows, :], fw_s.at[lax.rem(k, 2), c])

    acc[...] = jnp.zeros_like(acc)

    @pl.when(p == 0)
    def _():
        for c, rows in enumerate(chunks):
            start_block(c, rows)

    def send_inv():
        for d in range(1, NR):
            remote(
                inv.at[:, lanes(at_z(d))], inv_cols.at[lanes(z), :], inv_s.at[d - 1], inv_r.at[d - 1], (f, p, at_z(d))
            ).start()

    @pl.when(core == 0)
    def _():
        send_inv()

    @pl.when(low_send == -1)
    def _():
        send_low()

    @pl.when(p == 0)
    def _():
        for c, rows in enumerate(chunks):
            relay(by_lanes(gath, rows), g1_s.at[c], g1_r.at[c])

    load_f.wait()
    load_b.wait()

    @pl.loop(0, NP)
    def _(k):
        hi, lo = halves(stage[:, wide(k)])
        wh[:, wide(k)] = hi
        wl[:, wide(k)] = lo

    @pl.when(core == 1)
    def _():
        send_inv()

    owner_row = jnp.broadcast_to(own[...], (W, W)).astype(F32)
    owner_col = owner_row.T
    first = lax.broadcasted_iota(jnp.int32, (W, W), 0)
    second = lax.broadcasted_iota(jnp.int32, (W, W), 1)
    earlier = jnp.where((owner_col == owner_row) & (first < second), 1.0, 0.0)
    position = jnp.sum(earlier, axis=0, keepdims=True)
    tile = owner_row[0:1, :] * (2 * CAP) + position
    row_id = lax.broadcasted_iota(jnp.int32, (peers * 2 * CAP, W), 0).astype(F32)
    pick[...] = jnp.concatenate(
        [jnp.where(row_id == tile, 1.0, 0.0), jnp.where(row_id == tile + CAP, 1.0, 0.0)], axis=1
    ).astype(BF16)

    load_i.wait()
    for d in range(1, NR):
        arrived(inv_cols.at[lanes(at_z(-d)), :], inv_r.at[d - 1])
    hi, lo = halves(inv_cols[...])
    inv_hl[:, pl.ds(0, W)] = hi
    inv_hl[:, pl.ds(W, W)] = lo

    @pl.loop(0, NP)
    def _(k):
        lead, direct = role(k)
        block = solved.at[k]
        par_k = lax.rem(k, 2)

        @pl.when((p == k) & jnp.logical_not(folds))
        def _():
            @pl.when(k > 0)
            def _():
                for c, rows in enumerate(chunks):
                    relay(by_lanes(gath, rows), g1_s.at[c], g1_r.at[c])

            for c, rows in enumerate(chunks):
                mine[rows, :] = gathered(c, rows)
                send_solved(k, c, rows)

        for c, rows in enumerate(chunks):
            piece = by_lanes(block, rows)

            @pl.when((core == lead) & jnp.logical_not(direct))
            def _():
                arrived(piece(z), ag_r.at[k, c, 8])
                spread(piece, piece(z), ag_s.at[par_k, c], ag_r.at[k, c])

        for c, rows in enumerate(chunks):

            @pl.when(core == lead)
            def _():
                relay(by_lanes(block, rows), ag_s.at[par_k, c], ag_r.at[k, c])

            @pl.when((p == k + 1) & folds)
            def _():
                relay(by_lanes(gath, rows), g1_s.at[c], g1_r.at[c])

        for c, rows in enumerate(chunks):

            @pl.when((p == k + 1) & folds)
            def _():
                based[rows, :] = gathered(c, rows)

            @pl.when(core == lead)
            def _():
                piece = by_lanes(block, rows)

                @pl.when(direct)
                def _():
                    arrived(piece(z), ag_r.at[k, c, 8])

                finish(piece, ag_r.at[k, c])
                remote(
                    block.at[rows, :], block.at[rows, :], fw_s.at[par_k, c], fw_r.at[k, c], (f, col * 2 + 1 - lead, z)
                ).start()

            @pl.when(core != lead)
            def _():
                arrived(block.at[rows, :], fw_r.at[k, c])

            hi, lo = halves(block[rows, :])
            both = mul(jnp.concatenate([hi, lo], axis=0), wh[:, wide(k)], NT)
            term = both[:rows.size] + both[rows.size:] + mul(hi, wl[:, wide(k)], NT)

            @pl.when((p == k + 1) & folds)
            def _():
                mine[rows, :] = based[rows, :] - term[:, :W]
                send_solved(k + 1, c, rows)

            acc[rows, :] += term

            @pl.when(jnp.where(folds, p == k + 2, p == k + 1))
            def _():
                start_block(c, rows)

        @pl.when(low_send == k)
        def _():
            send_low()

        @pl.when(low_relay == k)
        def _():
            relay(by_rows(low), low_s, low_r)

        @pl.when(low_use == k)
        def _():
            finish(by_rows(low), low_r)
            pltpu.make_async_copy(low.at[lanes(z), :], low.at[lanes(z), :], load_sem.at[3]).wait()
            ih, il = halves(inv_cols[...].T)

            @pl.loop(0, span // (2 * W))
            def _(i):
                some = pl.ds(pl.multiple_of(i * 2 * W, 2 * W), 2 * W)
                hi, lo = halves(low[:, some])
                hi, lo = halves(mul(ih, hi, NN) + mul(il, hi, NN) + mul(ih, lo, NN))
                into = pl.ds(pl.multiple_of((p - 1) * span + i * 2 * W, 2 * W), 2 * W)
                wh[pl.ds(0, W), into] = hi
                wl[pl.ds(0, W), into] = lo

        sent_block(k - 1, k > 0)

    half = mine.shape[0] // 2
    update = brhs[...] - acc[:, pl.ds(W, W)]
    tail = jnp.where(
        lax.broadcasted_iota(jnp.int32, (W - half, W), 0) == 0,
        jnp.broadcast_to(slot[...], (W - half, W)).astype(F32),
        0.0,
    )
    ext = jnp.concatenate(
        [
            jnp.concatenate([update[:half], tail], axis=0),
            jnp.concatenate([update[half:], tail], axis=0),
        ],
        axis=1,
    )
    hi, lo = halves(ext)
    tosend[...] = mul(pick[...], hi, NT) + mul(pick[...], lo, NT)

    def tiles(i):
        return pl.ds(pl.multiple_of(i * 2 * CAP, 2 * CAP), 2 * CAP)

    @pl.loop(1, peers)
    def _(i):
        t = lax.rem(me + i, peers)
        remote(
            tosend.at[tiles(t), :], got.at[tiles(me), :], own_s.at[i], own_r.at[i],
            (f, t // NR, lax.rem(t, NR)),
        ).start()

    got[tiles(me), :] = tosend[tiles(me), :]

    for d in range(1, NR):
        arrived(inv_cols.at[lanes(z), :], inv_s.at[d - 1])
    for c, rows in enumerate(chunks):
        piece = by_lanes(gath, rows)
        sent_near(piece, g1_s.at[c])
        sent_far(piece, g1_s.at[c])
        for i in range(4, 8):
            arrived(mine.at[rows, :], st_s.at[c, i])

        @pl.when(core == 0)
        def _():
            for i in range(4):
                arrived(mine.at[rows, :], st_s.at[c, i])

    @pl.when(folds)
    def _():
        sent_near(by_rows(low), low_s)
        sent_far(by_rows(low), low_s)

    sent_block(jnp.int32(NP - 1), True)

    @pl.loop(1, peers)
    def _(i):
        t = lax.rem(me + peers - i, peers)
        arrived(got.at[tiles(t), :], own_r.at[i])

    flat = got[...].T
    slots = flat[half:half + 1, :]
    hits = jnp.where(
        slots == lax.broadcasted_iota(jnp.int32, (par.shape[1], peers * 2 * CAP), 0).astype(F32), 1.0, 0.0
    ).astype(BF16)
    which = lax.rem(lax.broadcasted_iota(jnp.int32, (W, peers * 2 * CAP), 1) // CAP, 2)
    both = jnp.concatenate([jnp.where(which == 0, flat, 0.0), jnp.where(which == 1, flat, 0.0)], axis=0)
    hi, lo = halves(both)
    part[...] = mul(hi, hits, NT) + mul(lo, hits, NT)

    band = 2 * W // fronts

    def bands(i):
        return pl.ds(pl.multiple_of(i * band, band), band)

    for i in range(1, fronts):
        t = lax.rem(f + i, fronts)
        remote(part.at[bands(t), :], quarters.at[i - 1], rs_s.at[i - 1], rs_r.at[i - 1], (t, p, z)).start()
    @pl.loop(1, peers)
    def _(i):
        arrived(tosend.at[tiles(0), :], own_s.at[i])

    for i in range(1, fronts):
        arrived(quarters.at[i - 1], rs_r.at[i - 1])
    total = part[bands(f), :]
    for i in range(1, fronts):
        total = total + quarters[i - 1]
    summed[bands(f), :] = total
    for i in range(1, fronts):
        t = lax.rem(f + i, fronts)
        remote(summed.at[bands(f), :], summed.at[bands(f), :], fa_s.at[i - 1], fa_r.at[i - 1], (t, p, z)).start()
    out_sol[...] = mine[...]
    for i in range(1, fronts):
        arrived(quarters.at[i - 1], rs_s.at[i - 1])
    for i in range(1, fronts):
        arrived(summed.at[bands(lax.rem(f + fronts - i, fronts)), :], fa_r.at[i - 1])
    out_par[0:half, :] = par[0:half, :] + summed[0:half, :]
    out_par[half:2 * half, :] = par[half:2 * half, :] + summed[W:W + half, :]
    for i in range(1, fronts):
        arrived(part.at[bands(f), :], fa_s.at[i - 1])


def shards(factor, inv_diag, boundary, rhs, boundary_rhs, owner, slot, parent_in):
    fronts = lax.axis_size("front")
    sources = rhs.shape[1]
    depth = factor.shape[3]
    span = NR * W
    rows = parent_in.shape[1]
    size = (sources // 4 + 15) // 16 * 16
    cuts = [0, *range(sources - (sources - 1) // size * size, sources + 1, size)]
    chunks = tuple(pl.ds(i, j - i) for i, j in zip(cuts, cuts[1:]))
    ns = len(chunks)
    any_spec, vmem = pl.BlockSpec(memory_space=pl.ANY), pl.BlockSpec(memory_space=pltpu.VMEM)
    dma = pltpu.SemaphoreType.DMA
    return pl.pallas_call(
        functools.partial(kernel, chunks, fronts),
        out_shape=(
            jax.ShapeDtypeStruct((sources, W), F32),
            jax.ShapeDtypeStruct((sources, rows), F32),
        ),
        in_specs=[any_spec] * 3 + [vmem] * 5,
        out_specs=(vmem, vmem),
        scratch_shapes=[
            pltpu.VMEM((2 * W, depth), F32),
            pltpu.VMEM((2 * W, depth), BF16),
            pltpu.VMEM((2 * W, depth), BF16),
            pltpu.VMEM((span, W), F32),
            pltpu.VMEM((span, 2 * W), BF16),
            pltpu.VMEM((span, span), F32),
            pltpu.VMEM((sources, span), F32),
            pltpu.VMEM((sources, W), F32),
            pltpu.VMEM((NP, sources, span), F32),
            pltpu.VMEM((sources, W), F32),
            pltpu.VMEM((sources, 2 * W), F32),
            pltpu.VMEM((NP * NR * 2 * CAP, 2 * W), BF16),
            pltpu.VMEM((NP * NR * 2 * CAP, W), F32),
            pltpu.VMEM((NP * NR * 2 * CAP, W), F32),
            pltpu.VMEM((2 * W, rows), F32),
            pltpu.VMEM((max(1, fronts - 1), 2 * W // fronts, rows), F32),
            pltpu.VMEM((2 * W, rows), F32),
            dma((4,)),
            dma((NR - 1,)),
            dma((NR - 1,)),
            dma((8,)),
            dma((8,)),
            dma((ns, 8)),
            dma((ns, 8)),
            dma((ns, 8)),
            dma((2, ns, 8)),
            dma((NP, ns, 9)),
            dma((2, ns)),
            dma((NP, ns)),
            dma((NP * NR,)),
            dma((NP * NR,)),
            dma((fronts,)),
            dma((fronts,)),
            dma((fronts,)),
            dma((fronts,)),
        ],
        compiler_params=pltpu.CompilerParams(collective_id=0, has_side_effects=True, vmem_limit_bytes=60 << 20),
    )(factor[0, 0], boundary[0], inv_diag[0, 0], rhs[0], boundary_rhs[0], owner[:, :, 0], slot, parent_in)


def body(*args):
    solved, parent = shards(*args)
    return solved[None], parent


def solution(mesh):
    placed = (
        P("front", "pivot", "rows", None),
        P("front", "pivot", "rows", None),
        P("front", ("pivot", "rows"), None),
        P("front", None, ("pivot", "rows")),
        P("front", None, ("pivot", "rows")),
        P("front", ("pivot", "rows"), None),
        P("front", ("pivot", "rows")),
        P(None, ("pivot", "rows")),
    )
    return jax.shard_map(
        body,
        mesh=mesh,
        in_specs=placed,
        out_specs=(P("front", None, ("pivot", "rows")), P(None, ("pivot", "rows"))),
        check_vma=False,
    )
```
